32 devices in a mesh: row: 4 (over y, x), col: 8 (over z, core).
Axes of the slice: x: 2, y: 2, z: 4, core: 2. Of those that a mesh axis runs over, the one named last changes fastest.
Arguments:
- points: bfloat16 [8192, 256], P(('row', 'col')), may hold values from -0.4 to 0.4, as said below
- spread: float32 [8192], P(('row', 'col')), may hold values from 1 to 12
- vectors: bfloat16 [8192, 64], P(('row', 'col')), may hold values from -6 to 6
Outputs:
- product: float32 [8192, 64], P(('row', 'col'))
The draws below stay inside these ranges and needn't reach their ends.
Inputs may be any that keep to these rules, and one draw needn't show every extreme that they name: `points`: embedding entries are real values of order 0.1.
All inputs are finite; a program needn't handle non-finite values.
Results may differ from the reference program's by a relative error of at most 0.0085.
Values may be sent and summed in bfloat16 or wider, within the bound.
A program may use at most 128 MiB of HBM per device.

```python
import math
import jax
import jax.numpy as jnp
from jax import lax

F = 256
K = 64
NPTS = 8192


def draw_points(key, part):
    first_key = jax.random.fold_in(jax.random.fold_in(key, 17), 0)
    base = jnp.clip(jax.random.normal(first_key, (NPTS, F), jnp.float32), -6.0, 6.0)
    return (base * 0.0625).astype(jnp.bfloat16)


def levels(key, extent, shards, least, largest):
    loudness, own = 1.0, jax.random.fold_in(key, 6)
    for dim, shards_of in shards:
        steps = jnp.exp(jax.random.uniform(jax.random.fold_in(own, dim), (shards_of,), jnp.float32, least / len(shards), largest / len(shards)))
        loudness = loudness * jnp.repeat(steps, extent[dim] // shards_of).reshape([-1 if axis == dim else 1 for axis in range(len(extent))])
    return loudness


def scatter_about(stream_key, extent, width, reach, cuts=(), kind=jnp.bfloat16):
    values = width * jax.random.normal(stream_key, extent, jnp.float32)
    if cuts:
        values = values * levels(stream_key, extent, cuts, -0.22, 0.18)
    return jnp.clip(values, -reach, reach).astype(kind)


def setup_inputs(seed: int = 0) -> dict:
    arg_keys = jax.random.split(jax.random.key(seed), 4)
    points = draw_points(jax.random.fold_in(arg_keys[3], 71), 0)
    spread = jnp.clip(jnp.exp(math.log(12.0) - 2.4849066 * jax.random.uniform(arg_keys[1], (NPTS,), jnp.float32) ** levels(arg_keys[1], (NPTS,), ((0, 32),), -0.2, 0.2)), 1.0, 12.0)
    vectors = scatter_about(arg_keys[2], (NPTS, K), 1.0, 6.0, ((0, 32),))
    return {"points": points, "spread": spread, "vectors": vectors}


def reference(points, spread, vectors):
    total_rows = points.shape[0]
    block_rows = min(1024, total_rows)
    count = total_rows // block_rows
    point_f = points.astype(jnp.float32)
    squares = jnp.sum(point_f * point_f, axis=1)
    col_ids = jnp.arange(total_rows, dtype=jnp.int32)
    vec_f = vectors.astype(jnp.float32)

    def one_block(carry, index):
        start = (index * block_rows).astype(jnp.int32)
        rows = lax.dynamic_slice_in_dim(points, start, block_rows, 0)
        row_sq = lax.dynamic_slice_in_dim(squares, start, block_rows, 0)
        row_bw = lax.dynamic_slice_in_dim(spread, start, block_rows, 0)
        row_vec = lax.dynamic_slice_in_dim(vec_f, start, block_rows, 0)
        cross = jnp.dot(rows, points.T, preferred_element_type=jnp.float32)
        dist = row_sq[:, None] + squares[None, :] - 2.0 * cross
        row_ids = start + jnp.arange(block_rows, dtype=jnp.int32)
        kernel = jnp.where(row_ids[:, None] == col_ids[None, :], jnp.float32(0.0), jnp.exp(-row_bw[:, None] * dist))
        total = jnp.sum(kernel, axis=1)
        norm = (kernel / total[:, None]).astype(jnp.bfloat16)
        norm_f = norm.astype(jnp.float32)
        forward = jnp.dot(norm, vectors, preferred_element_type=jnp.float32)
        carry = carry + jnp.dot(norm_f.T, row_vec, preferred_element_type=jnp.float32)
        return carry, forward

    start_carry = jnp.zeros((total_rows, vectors.shape[1]), jnp.float32)
    backward, forwards = lax.scan(one_block, start_carry, jnp.arange(count, dtype=jnp.int32))
    forward = forwards.reshape(total_rows, vectors.shape[1])
    return 0.5 * (forward + backward)
```

```python
import functools
import math

import jax
import jax.numpy as jnp
from jax import lax
from jax.experimental import pallas as pl
from jax.experimental.pallas import tpu as pltpu
from jax.sharding import PartitionSpec as P

MESH = pl.DeviceIdType.MESH
LOG2E = math.log2(math.e)
VMEM_SPEC = pl.BlockSpec(memory_space=pltpu.VMEM)
ANY_SPEC = pl.BlockSpec(memory_space=pl.ANY)
HEAD = 16
UNROLL = 8
NT = (((1,), (1,)), ((), ()))


def terms(value):
    high = value.astype(jnp.bfloat16)
    rest = value - high.astype(jnp.float32)
    middle = rest.astype(jnp.bfloat16)
    return [high, middle, (rest - middle.astype(jnp.float32)).astype(jnp.bfloat16)]


def untangle(head):
    head = head.astype(jnp.float32)
    return head[0:1] + head[1:2] + head[2:3], head[3:4] + head[4:5] + head[5:6]


def plan(n_rows, n_cols):
    if (n_rows, n_cols) == (4, 8):
        return [(0, 0), (1, 0), (0, 2), (1, 2)], [(0, 0), (2, 0), (0, 4), (2, 4)], True
    return [(m, 0) for m in range(n_rows)], [(0, 2 * k) for k in range(n_cols // 2)], False


def kernel(
    n_rows, n_cols, pts_ref, bw_ref, vec_ref, out_ref,
    blk, crs, crs_col, direct, mirror, vec_all, part, t_in, inv,
    fwd_out, fwd_in, rev_out, rev_in,
    js, jr, ss, sr, cs, cr, ts, tr, fs, fr, gs, gr, ls,
):
    share, width = pts_ref.shape
    k_vec = vec_ref.shape[0]
    f32, bf16 = jnp.float32, jnp.bfloat16
    firsts, seconds, relayed = plan(n_rows, n_cols)
    half = share // 2
    chunks = [(0, HEAD + half), (HEAD + half, half), (HEAD + share, k_vec), (0, HEAD + share), (0, HEAD + share + k_vec)]
    VECS, WHOLE, ALL = 2, 3, 4
    row = lax.axis_index("row")
    col = lax.axis_index("col")

    def peer(offset):
        return {"row": lax.bitwise_xor(row, offset[0]), "col": lax.bitwise_xor(col, offset[1])}

    def second_at(q):
        return seconds[q // 2][0], seconds[q // 2][1] ^ (q % 2)

    if relayed:
        place = col % 2 + 2 * (row // 2) + 4 * (col // 4)
        greeted = [(0, 4), (2, 0), (1, 0), (0, 2), (0, 1)]
    else:
        place = col
        greeted = firsts[1:] + seconds[1:] + [(0, 1)]
    barrier = pltpu.get_barrier_semaphore()
    for offset in greeted:
        pl.semaphore_signal(barrier, inc=1, device_id=peer(offset), device_id_type=MESH)

    loads = [
        pltpu.make_async_copy(pts_ref, crs.at[0, pl.ds(HEAD, share)], ls.at[0]),
        pltpu.make_async_copy(pts_ref, blk.at[0, pl.ds(HEAD, share)], ls.at[1]),
        pltpu.make_async_copy(vec_ref, blk.at[0, pl.ds(HEAD + share, k_vec)], ls.at[2]),
    ]
    for load in loads:
        load.start()
    loads[0].wait()
    own = crs[0, HEAD:].astype(f32)
    half_sq = 0.5 * jnp.sum(own * own, axis=1, keepdims=True)
    wide = jnp.transpose(jnp.broadcast_to(half_sq, (share, 128)))
    head = jnp.concatenate(
        [t.astype(f32) for t in terms(bw_ref[...] * (2.0 * LOG2E)) + terms(wide[0:1])]
        + [jnp.zeros((HEAD - 6, share), f32)],
        axis=0,
    ).astype(bf16)
    blk[0, 0:HEAD] = head
    crs[0, 0:HEAD] = head
    part[...] = jnp.zeros_like(part)
    loads[1].wait()
    loads[2].wait()
    pl.semaphore_wait(barrier, len(greeted))

    started = []

    def start(copy):
        copy.start()
        started.append(copy)

    def j_copy(src, dst, c, offset):
        rows = pl.ds(*chunks[c])
        return pltpu.make_async_remote_copy(
            src_ref=blk.at[2 * src, rows], dst_ref=blk.at[2 * dst, rows],
            send_sem=js.at[dst, c], recv_sem=jr.at[dst, c],
            device_id=peer(offset), device_id_type=MESH,
        )

    def s_copy(k, c):
        rows = pl.ds(*chunks[c])
        return pltpu.make_async_remote_copy(
            src_ref=blk.at[2 * k, rows], dst_ref=blk.at[2 * k + 1, rows],
            send_sem=ss.at[k, c], recv_sem=sr.at[k, c],
            device_id=peer((0, 1)), device_id_type=MESH,
        )

    def c_copy(src, dst, c, offset):
        rows = pl.ds(*chunks[c])
        return pltpu.make_async_remote_copy(
            src_ref=crs.at[src, rows], dst_ref=crs.at[dst, rows],
            send_sem=cs.at[dst, c], recv_sem=cr.at[dst, c],
            device_id=peer(offset), device_id_type=MESH,
        )

    def j_wait(k, c):
        j_copy(0, k, c, seconds[k]).wait_recv()

    def s_wait(k, c):
        s_copy(k, c).wait_recv()

    def c_wait(m, c):
        c_copy(0, m, c, firsts[m]).wait_recv()

    def column(m):
        spread_row, half_row = untangle(crs[m, 0:HEAD])
        padded = jnp.concatenate([spread_row, half_row, jnp.zeros((6, share), f32)], axis=0)
        crs_col[m] = jnp.transpose(padded)

    everything = (0, share)

    def tile(m, q, i_part=everything, j_part=everything, diagonal=False):
        i0, ni = i_part
        j0, nj = j_part
        cols = crs_col[m, i0 : i0 + ni]
        arow, hrow = untangle(blk[q, 0:HEAD, j0 : j0 + nj])
        cross = lax.dot_general(
            crs[m, HEAD + i0 : HEAD + i0 + ni], blk[q, HEAD + j0 : HEAD + j0 + nj], NT,
            preferred_element_type=f32,
        )
        near = (cross - cols[:, 1:2]) - hrow
        first = jnp.exp2(near * cols[:, 0:1])
        second = jnp.exp2(near * arow)
        if diagonal:
            same = lax.broadcasted_iota(jnp.int32, (ni, nj), 0) == lax.broadcasted_iota(
                jnp.int32, (ni, nj), 1
            )
            first = jnp.where(same, 0.0, first)
            second = jnp.where(same, 0.0, second)
        where = pl.ds(pl.multiple_of(q * share + j0, math.gcd(share, nj)), nj)
        direct[m, i0 : i0 + ni, where] = first.astype(bf16)
        mirror[m, i0 : i0 + ni, where] = second.astype(bf16)
        at = lax.bitwise_xor(place, q)
        part[at, :, j0 : j0 + nj] += jnp.sum(second, axis=0, keepdims=True)

    def tiles(ms, qs, i_part=everything, j_part=everything):
        count = (ms[1] - ms[0]) * (qs[1] - qs[0])

        def body(index, carry):
            tile(ms[0] + index % (ms[1] - ms[0]), qs[0] + index // (ms[1] - ms[0]), i_part, j_part)
            return carry

        lax.fori_loop(0, count, body, 0, unroll=min(count, UNROLL))

    if relayed:
        for c in (0, 1):
            start(j_copy(0, 2, c, seconds[2]))
            start(c_copy(0, 2, c, firsts[2]))
        start(s_copy(0, ALL))
        start(c_copy(0, 1, WHOLE, firsts[1]))
        start(j_copy(0, 1, ALL, seconds[1]))
        column(0)
        tile(0, 0, diagonal=True)
        s_wait(0, ALL)
        tile(0, 1)
        for c in (0, 1):
            j_wait(2, c)
            start(j_copy(2, 3, c, seconds[1]))
            start(s_copy(2, c))
            c_wait(2, c)
            start(c_copy(2, 3, c, firsts[1]))
            if c == 0:
                j_wait(1, ALL)
                start(s_copy(1, ALL))
                c_wait(1, WHOLE)
                column(1)
                tiles((1, 2), (0, 2))
                tiles((0, 2), (2, 3))
                s_wait(1, ALL)
                tiles((0, 2), (3, 4))
        start(j_copy(0, 2, VECS, seconds[2]))
        start(j_copy(0, 3, VECS, seconds[3]))
        column(2)
        tiles((2, 3), (0, 4))
        tiles((0, 3), (4, 5))
        s_wait(2, 0)
        s_wait(2, 1)
        tiles((0, 3), (5, 6))
        for c in (0, 1):
            piece = (c * half, half)
            j_wait(3, c)
            start(s_copy(3, c))
            c_wait(3, c)
            if c == 0:
                column(3)
            tiles((3, 4), (0, 6), i_part=piece)
            tiles((0, 3), (6, 7), j_part=piece)
            if c == 1:
                tile(3, 6)
            s_wait(3, c)
            tiles((0, 3), (7, 8), j_part=piece)
        tile(3, 7)
        late = [2, 3]
    else:
        for k in range(1, len(seconds)):
            start(j_copy(0, k, WHOLE, seconds[k]))
        for m in range(1, n_rows):
            start(c_copy(0, m, WHOLE, firsts[m]))
        start(s_copy(0, ALL))
        column(0)
        tile(0, 0, diagonal=True)
        s_wait(0, ALL)
        tile(0, 1)
        for m in range(1, n_rows):
            c_wait(m, WHOLE)
            column(m)
        tiles((1, n_rows), (0, 2))
        for k in range(1, len(seconds)):
            j_wait(k, WHOLE)
            start(s_copy(k, WHOLE))
            start(j_copy(0, k, VECS, seconds[k]))
            tiles((0, n_rows), (2 * k, 2 * k + 1))
            s_wait(k, WHOLE)
            tiles((0, n_rows), (2 * k + 1, 2 * k + 2))
        late = list(range(1, len(seconds)))

    totals = []
    for x in range(n_cols - 1, 0, -1):
        copy = pltpu.make_async_remote_copy(
            src_ref=part, dst_ref=t_in.at[x], send_sem=ts.at[x], recv_sem=tr.at[x],
            device_id=peer(second_at(x)), device_id_type=MESH,
        )
        start(copy)
        totals.insert(0, copy)
    for k in late:
        j_wait(k, VECS)
        start(s_copy(k, VECS))
    for k in late:
        s_wait(k, VECS)
    for q in range(n_cols):
        vec_all[:, q * share : (q + 1) * share] = blk[q, HEAD + share :]

    def reduce_send(m, value, out, in_, send, recv):
        out[m] = value.astype(bf16)
        copy = pltpu.make_async_remote_copy(
            src_ref=out.at[m], dst_ref=in_.at[m], send_sem=send.at[m], recv_sem=recv.at[m],
            device_id=peer(firsts[m]), device_id_type=MESH,
        )
        start(copy)
        return copy

    def product(left, right):
        return lax.dot_general(left, right, NT, preferred_element_type=f32)

    order = list(range(n_rows - 1, 0, -1))
    fwd = {m: reduce_send(m, product(vec_all[...], direct[m]), fwd_out, fwd_in, fs, fr) for m in order}
    forward = product(vec_all[...], direct[0])

    total = part[...]
    for x in range(1, n_cols):
        totals[x - 1].wait_recv()
        total = total + t_in[x]
    inv[...] = 0.125 / total
    scaled = jnp.concatenate(
        [
            (vec_all[:, q * share : (q + 1) * share].astype(f32) * inv[lax.bitwise_xor(place, q)]).astype(bf16)
            for q in range(n_cols)
        ],
        axis=1,
    )
    rev = {m: reduce_send(m, product(scaled, mirror[m]), rev_out, rev_in, gs, gr) for m in order}
    reverse = product(scaled, mirror[0])
    for m in range(1, n_rows):
        fwd[m].wait_recv()
        forward = forward + fwd_in[m].astype(f32)
    forward = forward * inv[place]
    for copy in started:
        copy.wait_send()
    for m in range(1, n_rows):
        rev[m].wait_recv()
        reverse = reverse + rev_in[m].astype(f32)
    out_ref[...] = 4.0 * (forward + reverse)


def local(n_rows, n_cols, points, spread, vectors):
    share, width = points.shape
    k = vectors.shape[1]
    f32, bf16 = jnp.float32, jnp.bfloat16
    dma = pltpu.SemaphoreType.DMA
    n = n_cols // 2
    scratch = [
        pltpu.VMEM((n_cols, HEAD + share + k, width), bf16),
        pltpu.VMEM((n_rows, HEAD + share, width), bf16),
        pltpu.VMEM((n_rows, share, 8), f32),
        pltpu.VMEM((n_rows, share, n_cols * share), bf16),
        pltpu.VMEM((n_rows, share, n_cols * share), bf16),
        pltpu.VMEM((k, n_cols * share), bf16),
        pltpu.VMEM((n_cols, 1, share), f32),
        pltpu.VMEM((n_cols, n_cols, 1, share), f32),
        pltpu.VMEM((n_cols, 1, share), f32),
    ] + [pltpu.VMEM((n_rows, k, share), bf16)] * 4
    scratch += [dma((n, 5))] * 4 + [dma((n_rows, 4))] * 2 + [dma((n_cols,))] * 2
    scratch += [dma((n_rows,))] * 4 + [dma((3,))]
    out = pl.pallas_call(
        functools.partial(kernel, n_rows, n_cols),
        out_shape=pltpu.VMEM((k, share), f32),
        in_specs=[ANY_SPEC, VMEM_SPEC, ANY_SPEC],
        out_specs=VMEM_SPEC,
        scratch_shapes=scratch,
        compiler_params=pltpu.CompilerParams(
            collective_id=0, has_side_effects=True, vmem_limit_bytes=58 * 1024 * 1024
        ),
    )(points, spread.reshape(1, share), vectors.T)
    return out.T


def solution(mesh):
    placed = (P(("row", "col"), None), P(("row", "col")), P(("row", "col"), None))
    return jax.shard_map(
        functools.partial(local, mesh.shape["row"], mesh.shape["col"]),
        mesh=mesh, in_specs=placed, out_specs=P(("row", "col"), None), check_vma=False,
    )
```

```python
import functools
import math

import jax
import jax.numpy as jnp
from jax import lax
from jax.experimental import pallas as pl
from jax.experimental.pallas import tpu as pltpu
from jax.sharding import PartitionSpec as P

MESH = pl.DeviceIdType.MESH
LOG2E = math.log2(math.e)
VMEM_SPEC = pl.BlockSpec(memory_space=pltpu.VMEM)
ANY_SPEC = pl.BlockSpec(memory_space=pl.ANY)
HEAD = 16
UNROLL = 8
NT = (((1,), (1,)), ((), ()))


def terms(value):
    high = value.astype(jnp.bfloat16)
    rest = value - high.astype(jnp.float32)
    middle = rest.astype(jnp.bfloat16)
    return [high, middle, (rest - middle.astype(jnp.float32)).astype(jnp.bfloat16)]


def untangle(head):
    head = head.astype(jnp.float32)
    return head[0:1] + head[1:2] + head[2:3], head[3:4] + head[4:5] + head[5:6]


def plan(n_rows, n_cols):
    if (n_rows, n_cols) == (4, 8):
        return [(0, 0), (1, 0), (0, 2), (1, 2)], [(0, 0), (2, 0), (0, 4), (2, 4)], True
    return [(m, 0) for m in range(n_rows)], [(0, 2 * k) for k in range(n_cols // 2)], False


def kernel(
    n_rows, n_cols, pts_ref, bw_ref, vec_ref, out_ref,
    blk, crs, crs_col, direct, mirror, vec_all, part, t_in, inv,
    fwd_out, fwd_in, rev_out, rev_in,
    bw, js, jr, ss, sr, cs, cr, ts, tr, fs, fr, gs, gr, ls,
):
    share, width = pts_ref.shape
    k_vec = vec_ref.shape[0]
    f32, bf16 = jnp.float32, jnp.bfloat16
    firsts, seconds, relayed = plan(n_rows, n_cols)
    half = share // 2
    chunks = [(0, HEAD + half), (HEAD + half, half), (HEAD + share, k_vec), (0, HEAD + share), (0, HEAD + share + k_vec)]
    VECS, WHOLE, ALL = 2, 3, 4
    row = lax.axis_index("row")
    col = lax.axis_index("col")

    def peer(offset):
        return {"row": lax.bitwise_xor(row, offset[0]), "col": lax.bitwise_xor(col, offset[1])}

    def second_at(q):
        return seconds[q // 2][0], seconds[q // 2][1] ^ (q % 2)

    if relayed:
        place = col % 2 + 2 * (row // 2) + 4 * (col // 4)
        greeted = [(0, 4), (2, 0), (1, 0), (0, 2), (0, 1)]
    else:
        place = col
        greeted = firsts[1:] + seconds[1:] + [(0, 1)]
    barrier = pltpu.get_barrier_semaphore()
    for offset in greeted:
        pl.semaphore_signal(barrier, inc=1, device_id=peer(offset), device_id_type=MESH)

    loads = [
        pltpu.make_async_copy(pts_ref, crs.at[0, pl.ds(HEAD, share)], ls.at[0]),
        pltpu.make_async_copy(pts_ref, blk.at[0, pl.ds(HEAD, share)], ls.at[1]),
        pltpu.make_async_copy(bw_ref, bw, ls.at[3]),
        pltpu.make_async_copy(vec_ref, blk.at[0, pl.ds(HEAD + share, k_vec)], ls.at[2]),
    ]
    for load in loads:
        load.start()
    loads[0].wait()
    loads[2].wait()
    own = crs[0, HEAD:].astype(f32)
    half_sq = 0.5 * jnp.sum(own * own, axis=1, keepdims=True)
    wide = jnp.transpose(jnp.broadcast_to(half_sq, (share, 128)))
    head = jnp.concatenate(
        [t.astype(f32) for t in terms(bw[...] * (2.0 * LOG2E)) + terms(wide[0:1])]
        + [jnp.zeros((HEAD - 6, share), f32)],
        axis=0,
    ).astype(bf16)
    blk[0, 0:HEAD] = head
    crs[0, 0:HEAD] = head
    part[...] = jnp.zeros_like(part)
    loads[1].wait()
    loads[3].wait()
    pl.semaphore_wait(barrier, len(greeted))

    started = []

    def start(copy):
        copy.start()
        started.append(copy)

    def j_copy(src, dst, c, offset):
        rows = pl.ds(*chunks[c])
        return pltpu.make_async_remote_copy(
            src_ref=blk.at[2 * src, rows], dst_ref=blk.at[2 * dst, rows],
            send_sem=js.at[dst, c], recv_sem=jr.at[dst, c],
            device_id=peer(offset), device_id_type=MESH,
        )

    def s_copy(k, c):
        rows = pl.ds(*chunks[c])
        return pltpu.make_async_remote_copy(
            src_ref=blk.at[2 * k, rows], dst_ref=blk.at[2 * k + 1, rows],
            send_sem=ss.at[k, c], recv_sem=sr.at[k, c],
            device_id=peer((0, 1)), device_id_type=MESH,
        )

    def c_copy(src, dst, c, offset):
        rows = pl.ds(*chunks[c])
        return pltpu.make_async_remote_copy(
            src_ref=crs.at[src, rows], dst_ref=crs.at[dst, rows],
            send_sem=cs.at[dst, c], recv_sem=cr.at[dst, c],
            device_id=peer(offset), device_id_type=MESH,
        )

    def j_wait(k, c):
        j_copy(0, k, c, seconds[k]).wait_recv()

    def s_wait(k, c):
        s_copy(k, c).wait_recv()

    def c_wait(m, c):
        c_copy(0, m, c, firsts[m]).wait_recv()

    def column(m):
        spread_row, half_row = untangle(crs[m, 0:HEAD])
        padded = jnp.concatenate([spread_row, half_row, jnp.zeros((6, share), f32)], axis=0)
        crs_col[m] = jnp.transpose(padded)

    everything = (0, share)

    def tile(m, q, i_part=everything, j_part=everything, diagonal=False):
        i0, ni = i_part
        j0, nj = j_part
        cols = crs_col[m, i0 : i0 + ni]
        arow, hrow = untangle(blk[q, 0:HEAD, j0 : j0 + nj])
        cross = lax.dot_general(
            crs[m, HEAD + i0 : HEAD + i0 + ni], blk[q, HEAD + j0 : HEAD + j0 + nj], NT,
            preferred_element_type=f32,
        )
        near = (cross - cols[:, 1:2]) - hrow
        first = jnp.exp2(near * cols[:, 0:1])
        second = jnp.exp2(near * arow)
        if diagonal:
            same = lax.broadcasted_iota(jnp.int32, (ni, nj), 0) == lax.broadcasted_iota(
                jnp.int32, (ni, nj), 1
            )
            first = jnp.where(same, 0.0, first)
            second = jnp.where(same, 0.0, second)
        where = pl.ds(pl.multiple_of(q * share + j0, math.gcd(share, nj)), nj)
        direct[m, i0 : i0 + ni, where] = first.astype(bf16)
        mirror[m, i0 : i0 + ni, where] = second.astype(bf16)
        at = lax.bitwise_xor(place, q)
        part[at, :, j0 : j0 + nj] += jnp.sum(second, axis=0, keepdims=True)

    def tiles(ms, qs, i_part=everything, j_part=everything):
        count = (ms[1] - ms[0]) * (qs[1] - qs[0])

        def body(index, carry):
            tile(ms[0] + index % (ms[1] - ms[0]), qs[0] + index // (ms[1] - ms[0]), i_part, j_part)
            return carry

        lax.fori_loop(0, count, body, 0, unroll=min(count, UNROLL))

    if relayed:
        for c in (0, 1):
            start(j_copy(0, 2, c, seconds[2]))
            start(c_copy(0, 2, c, firsts[2]))
        start(s_copy(0, ALL))
        start(c_copy(0, 1, WHOLE, firsts[1]))
        start(j_copy(0, 1, ALL, seconds[1]))
        column(0)
        tile(0, 0, diagonal=True)
        s_wait(0, ALL)
        tile(0, 1)
        for c in (0, 1):
            j_wait(2, c)
            start(j_copy(2, 3, c, seconds[1]))
            start(s_copy(2, c))
            c_wait(2, c)
            start(c_copy(2, 3, c, firsts[1]))
            if c == 0:
                j_wait(1, ALL)
                start(s_copy(1, ALL))
                c_wait(1, WHOLE)
                start(j_copy(0, 2, VECS, seconds[2]))
                start(j_copy(0, 3, VECS, seconds[3]))
                column(1)
                tiles((1, 2), (0, 2))
                tiles((0, 2), (2, 3))
                s_wait(1, ALL)
                tiles((0, 2), (3, 4))
        column(2)
        tiles((2, 3), (0, 4))
        tiles((0, 3), (4, 5))
        s_wait(2, 0)
        s_wait(2, 1)
        tiles((0, 3), (5, 6))
        for c in (0, 1):
            piece = (c * half, half)
            j_wait(3, c)
            start(s_copy(3, c))
            c_wait(3, c)
            if c == 0:
                column(3)
            tiles((3, 4), (0, 6), i_part=piece)
            tiles((0, 3), (6, 7), j_part=piece)
            if c == 1:
                for k in (2, 3):
                    j_wait(k, VECS)
                    start(s_copy(k, VECS))
                tile(3, 6)
            s_wait(3, c)
            tiles((0, 3), (7, 8), j_part=piece)
        tile(3, 7)
        late = [2, 3]
    else:
        for k in range(1, len(seconds)):
            start(j_copy(0, k, WHOLE, seconds[k]))
        for m in range(1, n_rows):
            start(c_copy(0, m, WHOLE, firsts[m]))
        start(s_copy(0, ALL))
        column(0)
        tile(0, 0, diagonal=True)
        s_wait(0, ALL)
        tile(0, 1)
        for m in range(1, n_rows):
            c_wait(m, WHOLE)
            column(m)
        tiles((1, n_rows), (0, 2))
        for k in range(1, len(seconds)):
            j_wait(k, WHOLE)
            start(s_copy(k, WHOLE))
            start(j_copy(0, k, VECS, seconds[k]))
            tiles((0, n_rows), (2 * k, 2 * k + 1))
            s_wait(k, WHOLE)
            tiles((0, n_rows), (2 * k + 1, 2 * k + 2))
        late = list(range(1, len(seconds)))

    totals = []
    for x in range(n_cols - 1, 0, -1):
        copy = pltpu.make_async_remote_copy(
            src_ref=part, dst_ref=t_in.at[x], send_sem=ts.at[x], recv_sem=tr.at[x],
            device_id=peer(second_at(x)), device_id_type=MESH,
        )
        start(copy)
        totals.insert(0, copy)
    if not relayed:
        for k in late:
            j_wait(k, VECS)
            start(s_copy(k, VECS))
    for k in late:
        s_wait(k, VECS)
    for q in range(n_cols):
        vec_all[:, q * share : (q + 1) * share] = blk[q, HEAD + share :]

    def reduce_send(m, value, out, in_, send, recv):
        out[m] = value.astype(bf16)
        copy = pltpu.make_async_remote_copy(
            src_ref=out.at[m], dst_ref=in_.at[m], send_sem=send.at[m], recv_sem=recv.at[m],
            device_id=peer(firsts[m]), device_id_type=MESH,
        )
        start(copy)
        return copy

    def product(left, right):
        return lax.dot_general(left, right, NT, preferred_element_type=f32)

    order = list(range(n_rows - 1, 0, -1))
    fwd = {m: reduce_send(m, product(vec_all[...], direct[m]), fwd_out, fwd_in, fs, fr) for m in order}
    forward = product(vec_all[...], direct[0])

    total = part[...]
    for x in range(1, n_cols):
        totals[x - 1].wait_recv()
        total = total + t_in[x]
    inv[...] = 0.125 / total
    scaled = jnp.concatenate(
        [
            (vec_all[:, q * share : (q + 1) * share].astype(f32) * inv[lax.bitwise_xor(place, q)]).astype(bf16)
            for q in range(n_cols)
        ],
        axis=1,
    )
    rev = {m: reduce_send(m, product(scaled, mirror[m]), rev_out, rev_in, gs, gr) for m in order}
    reverse = product(scaled, mirror[0])
    for m in range(1, n_rows):
        fwd[m].wait_recv()
        forward = forward + fwd_in[m].astype(f32)
    forward = forward * inv[place]
    for copy in started:
        copy.wait_send()
    for m in range(1, n_rows):
        rev[m].wait_recv()
        reverse = reverse + rev_in[m].astype(f32)
    out_ref[...] = 4.0 * (forward + reverse)


def local(n_rows, n_cols, points, spread, vectors):
    share, width = points.shape
    k = vectors.shape[1]
    f32, bf16 = jnp.float32, jnp.bfloat16
    dma = pltpu.SemaphoreType.DMA
    n = n_cols // 2
    scratch = [
        pltpu.VMEM((n_cols, HEAD + share + k, width), bf16),
        pltpu.VMEM((n_rows, HEAD + share, width), bf16),
        pltpu.VMEM((n_rows, share, 8), f32),
        pltpu.VMEM((n_rows, share, n_cols * share), bf16),
        pltpu.VMEM((n_rows, share, n_cols * share), bf16),
        pltpu.VMEM((k, n_cols * share), bf16),
        pltpu.VMEM((n_cols, 1, share), f32),
        pltpu.VMEM((n_cols, n_cols, 1, share), f32),
        pltpu.VMEM((n_cols, 1, share), f32),
    ] + [pltpu.VMEM((n_rows, k, share), bf16)] * 4
    scratch += [pltpu.VMEM((1, share), f32)]
    scratch += [dma((n, 5))] * 4 + [dma((n_rows, 4))] * 2 + [dma((n_cols,))] * 2
    scratch += [dma((n_rows,))] * 4 + [dma((4,))]
    out = pl.pallas_call(
        functools.partial(kernel, n_rows, n_cols),
        out_shape=pltpu.VMEM((k, share), f32),
        in_specs=[ANY_SPEC, ANY_SPEC, ANY_SPEC],
        out_specs=VMEM_SPEC,
        scratch_shapes=scratch,
        compiler_params=pltpu.CompilerParams(
            collective_id=0, has_side_effects=True, vmem_limit_bytes=58 * 1024 * 1024
        ),
    )(points, spread.reshape(1, share), vectors.T)
    return out.T


def solution(mesh):
    placed = (P(("row", "col"), None), P(("row", "col")), P(("row", "col"), None))
    return jax.shard_map(
        functools.partial(local, mesh.shape["row"], mesh.shape["col"]),
        mesh=mesh, in_specs=placed, out_specs=P(("row", "col"), None), check_vma=False,
    )
```

```python
import functools
import math

import jax
import jax.numpy as jnp
from jax import lax
from jax.experimental import pallas as pl
from jax.experimental.pallas import tpu as pltpu
from jax.sharding import PartitionSpec as P

MESH = pl.DeviceIdType.MESH
LOG2E = math.log2(math.e)
VMEM_SPEC = pl.BlockSpec(memory_space=pltpu.VMEM)
ANY_SPEC = pl.BlockSpec(memory_space=pl.ANY)
HEAD = 16
UNROLL = 8
NT = (((1,), (1,)), ((), ()))


def terms(value):
    high = value.astype(jnp.bfloat16)
    rest = value - high.astype(jnp.float32)
    middle = rest.astype(jnp.bfloat16)
    return [high, middle, (rest - middle.astype(jnp.float32)).astype(jnp.bfloat16)]


def untangle(head):
    head = head.astype(jnp.float32)
    return head[0:1] + head[1:2] + head[2:3], head[3:4] + head[4:5] + head[5:6]


def plan(n_rows, n_cols):
    if (n_rows, n_cols) == (4, 8):
        return [(0, 0), (1, 0), (0, 2), (1, 2)], [(0, 0), (2, 1), (0, 5), (2, 4)], True
    return [(m, 0) for m in range(n_rows)], [(0, 2 * k) for k in range(n_cols // 2)], False


def kernel(
    n_rows, n_cols, pts_ref, bw_ref, vec_ref, out_ref,
    blk, crs, crs_col, direct, mirror, vec_all, part, t_in, inv,
    fwd_out, fwd_in, rev_out, rev_in,
    bw, js, jr, ss, sr, cs, cr, ts, tr, fs, fr, gs, gr, ls,
):
    share, width = pts_ref.shape
    k_vec = vec_ref.shape[0]
    f32, bf16 = jnp.float32, jnp.bfloat16
    firsts, seconds, relayed = plan(n_rows, n_cols)
    half = share // 2
    chunks = [(0, HEAD + half), (HEAD + half, half), (HEAD + share, k_vec), (0, HEAD + share), (0, HEAD + share + k_vec)]
    VECS, WHOLE, ALL = 2, 3, 4
    row = lax.axis_index("row")
    col = lax.axis_index("col")

    def peer(offset):
        return {"row": lax.bitwise_xor(row, offset[0]), "col": lax.bitwise_xor(col, offset[1])}

    def second_at(q):
        return seconds[q // 2][0], seconds[q // 2][1] ^ (q % 2)

    if relayed:
        y, far = row // 2, col // 4
        place = (col + y + far) % 2 + 2 * y + 4 * far
        greeted = [seconds[2], seconds[1], firsts[1], firsts[2], (0, 1)]
    else:
        place = col
        greeted = firsts[1:] + seconds[1:] + [(0, 1)]
    barrier = pltpu.get_barrier_semaphore()
    for offset in greeted:
        pl.semaphore_signal(barrier, inc=1, device_id=peer(offset), device_id_type=MESH)

    loads = [
        pltpu.make_async_copy(pts_ref, crs.at[0, pl.ds(HEAD, share)], ls.at[0]),
        pltpu.make_async_copy(pts_ref, blk.at[0, pl.ds(HEAD, share)], ls.at[1]),
        pltpu.make_async_copy(bw_ref, bw, ls.at[3]),
        pltpu.make_async_copy(vec_ref, blk.at[0, pl.ds(HEAD + share, k_vec)], ls.at[2]),
    ]
    for load in loads:
        load.start()
    loads[0].wait()
    loads[2].wait()
    own = crs[0, HEAD:].astype(f32)
    square = own * own
    high = square.astype(bf16)
    low = (square - high.astype(f32)).astype(bf16)
    halves = jnp.full((8, width), 0.5, bf16)
    wide = lax.dot_general(halves, high, NT, preferred_element_type=f32) + lax.dot_general(
        halves, low, NT, preferred_element_type=f32
    )
    head = jnp.concatenate(
        [t.astype(f32) for t in terms(bw[...] * (2.0 * LOG2E)) + terms(wide[0:1])]
        + [jnp.zeros((HEAD - 6, share), f32)],
        axis=0,
    ).astype(bf16)
    blk[0, 0:HEAD] = head
    crs[0, 0:HEAD] = head
    part[...] = jnp.zeros_like(part)
    loads[1].wait()
    loads[3].wait()
    pl.semaphore_wait(barrier, len(greeted))

    started = []

    def start(copy):
        copy.start()
        started.append(copy)

    def j_copy(src, dst, c, offset):
        rows = pl.ds(*chunks[c])
        return pltpu.make_async_remote_copy(
            src_ref=blk.at[2 * src, rows], dst_ref=blk.at[2 * dst, rows],
            send_sem=js.at[dst, c], recv_sem=jr.at[dst, c],
            device_id=peer(offset), device_id_type=MESH,
        )

    def s_copy(k, c):
        rows = pl.ds(*chunks[c])
        return pltpu.make_async_remote_copy(
            src_ref=blk.at[2 * k, rows], dst_ref=blk.at[2 * k + 1, rows],
            send_sem=ss.at[k, c], recv_sem=sr.at[k, c],
            device_id=peer((0, 1)), device_id_type=MESH,
        )

    def c_copy(src, dst, c, offset):
        rows = pl.ds(*chunks[c])
        return pltpu.make_async_remote_copy(
            src_ref=crs.at[src, rows], dst_ref=crs.at[dst, rows],
            send_sem=cs.at[dst, c], recv_sem=cr.at[dst, c],
            device_id=peer(offset), device_id_type=MESH,
        )

    def j_wait(k, c):
        j_copy(0, k, c, seconds[k]).wait_recv()

    def s_wait(k, c):
        s_copy(k, c).wait_recv()

    def c_wait(m, c):
        c_copy(0, m, c, firsts[m]).wait_recv()

    def column(m):
        spread_row, half_row = untangle(crs[m, 0:HEAD])
        padded = jnp.concatenate([spread_row, half_row, jnp.zeros((6, share), f32)], axis=0)
        crs_col[m] = jnp.transpose(padded)

    everything = (0, share)

    def tile(m, q, i_part=everything, j_part=everything, diagonal=False):
        i0, ni = i_part
        j0, nj = j_part
        cols = crs_col[m, i0 : i0 + ni]
        arow, hrow = untangle(blk[q, 0:HEAD, j0 : j0 + nj])
        cross = lax.dot_general(
            crs[m, HEAD + i0 : HEAD + i0 + ni], blk[q, HEAD + j0 : HEAD + j0 + nj], NT,
            preferred_element_type=f32,
        )
        near = (cross - cols[:, 1:2]) - hrow
        first = jnp.exp2(near * cols[:, 0:1])
        second = jnp.exp2(near * arow)
        if diagonal:
            same = lax.broadcasted_iota(jnp.int32, (ni, nj), 0) == lax.broadcasted_iota(
                jnp.int32, (ni, nj), 1
            )
            first = jnp.where(same, 0.0, first)
            second = jnp.where(same, 0.0, second)
        where = pl.ds(pl.multiple_of(q * share + j0, math.gcd(share, nj)), nj)
        direct[m, i0 : i0 + ni, where] = first.astype(bf16)
        mirror[m, i0 : i0 + ni, where] = second.astype(bf16)
        at = lax.bitwise_xor(place, q)
        part[at, :, j0 : j0 + nj] += jnp.sum(second, axis=0, keepdims=True)

    def tiles(ms, qs, i_part=everything, j_part=everything):
        count = (ms[1] - ms[0]) * (qs[1] - qs[0])

        def body(index, carry):
            tile(ms[0] + index % (ms[1] - ms[0]), qs[0] + index // (ms[1] - ms[0]), i_part, j_part)
            return carry

        lax.fori_loop(0, count, body, 0, unroll=min(count, UNROLL))

    if relayed:
        start(j_copy(0, 2, 0, seconds[2]))
        start(c_copy(0, 2, 0, firsts[2]))
        start(j_copy(0, 1, ALL, seconds[1]))
        start(c_copy(0, 1, WHOLE, firsts[1]))
        start(s_copy(0, ALL))
        start(j_copy(0, 2, 1, seconds[2]))
        start(c_copy(0, 2, 1, firsts[2]))
        column(0)
        tile(0, 0, diagonal=True)
        s_wait(0, ALL)
        tile(0, 1)
        for c in (0, 1):
            j_wait(2, c)
            start(j_copy(2, 3, c, seconds[1]))
            c_wait(2, c)
            start(c_copy(2, 3, c, firsts[1]))
            start(s_copy(2, c))
            if c == 0:
                j_wait(1, ALL)
                start(s_copy(1, ALL))
                c_wait(1, WHOLE)
                start(j_copy(0, 2, VECS, seconds[2]))
                column(1)
                tiles((1, 2), (0, 2))
                tiles((0, 2), (2, 3))
                s_wait(1, ALL)
                tiles((0, 2), (3, 4))
        column(2)
        tiles((2, 3), (0, 4))
        tiles((0, 3), (4, 5))
        s_wait(2, 0)
        s_wait(2, 1)
        tiles((0, 3), (5, 6))
        j_wait(2, VECS)
        start(j_copy(2, 3, VECS, seconds[1]))
        start(s_copy(2, VECS))
        for c in (0, 1):
            piece = (c * half, half)
            j_wait(3, c)
            start(s_copy(3, c))
            tiles((0, 3), (6, 7), j_part=piece)
            c_wait(3, c)
            if c == 0:
                column(3)
            tiles((3, 4), (0, 6), i_part=piece)
            if c == 1:
                tile(3, 6)
            s_wait(3, c)
            tiles((0, 3), (7, 8), j_part=piece)
        tile(3, 7)
        late = [2, 3]
    else:
        for k in range(1, len(seconds)):
            start(j_copy(0, k, WHOLE, seconds[k]))
        for m in range(1, n_rows):
            start(c_copy(0, m, WHOLE, firsts[m]))
        start(s_copy(0, ALL))
        column(0)
        tile(0, 0, diagonal=True)
        s_wait(0, ALL)
        tile(0, 1)
        for m in range(1, n_rows):
            c_wait(m, WHOLE)
            column(m)
        tiles((1, n_rows), (0, 2))
        for k in range(1, len(seconds)):
            j_wait(k, WHOLE)
            start(s_copy(k, WHOLE))
            start(j_copy(0, k, VECS, seconds[k]))
            tiles((0, n_rows), (2 * k, 2 * k + 1))
            s_wait(k, WHOLE)
            tiles((0, n_rows), (2 * k + 1, 2 * k + 2))
        late = list(range(1, len(seconds)))

    totals = []
    for x in range(n_cols - 1, 0, -1):
        copy = pltpu.make_async_remote_copy(
            src_ref=part, dst_ref=t_in.at[x], send_sem=ts.at[x], recv_sem=tr.at[x],
            device_id=peer(second_at(x)), device_id_type=MESH,
        )
        start(copy)
        totals.insert(0, copy)
    if not relayed:
        for k in late:
            j_wait(k, VECS)
            start(s_copy(k, VECS))
    if relayed:
        j_wait(3, VECS)
        start(s_copy(3, VECS))
    for k in late:
        s_wait(k, VECS)
    for q in range(n_cols):
        vec_all[:, q * share : (q + 1) * share] = blk[q, HEAD + share :]

    def reduce_send(m, value, out, in_, send, recv):
        out[m] = value.astype(bf16)
        copy = pltpu.make_async_remote_copy(
            src_ref=out.at[m], dst_ref=in_.at[m], send_sem=send.at[m], recv_sem=recv.at[m],
            device_id=peer(firsts[m]), device_id_type=MESH,
        )
        start(copy)
        return copy

    def product(left, right):
        return lax.dot_general(left, right, NT, preferred_element_type=f32)

    order = list(range(n_rows - 1, 0, -1))
    fwd = {m: reduce_send(m, product(vec_all[...], direct[m]), fwd_out, fwd_in, fs, fr) for m in order}
    forward = product(vec_all[...], direct[0])

    total = part[...]
    for x in range(1, n_cols):
        totals[x - 1].wait_recv()
        total = total + t_in[x]
    inv[...] = 0.125 / total
    scaled = jnp.concatenate(
        [
            (vec_all[:, q * share : (q + 1) * share].astype(f32) * inv[lax.bitwise_xor(place, q)]).astype(bf16)
            for q in range(n_cols)
        ],
        axis=1,
    )
    rev = {m: reduce_send(m, product(scaled, mirror[m]), rev_out, rev_in, gs, gr) for m in order}
    reverse = product(scaled, mirror[0])
    for m in range(1, n_rows):
        fwd[m].wait_recv()
        forward = forward + fwd_in[m].astype(f32)
    forward = forward * inv[place]
    for copy in started:
        copy.wait_send()
    for m in range(1, n_rows):
        rev[m].wait_recv()
        reverse = reverse + rev_in[m].astype(f32)
    out_ref[...] = 4.0 * (forward + reverse)


def local(n_rows, n_cols, points, spread, vectors):
    share, width = points.shape
    k = vectors.shape[1]
    f32, bf16 = jnp.float32, jnp.bfloat16
    dma = pltpu.SemaphoreType.DMA
    n = n_cols // 2
    scratch = [
        pltpu.VMEM((n_cols, HEAD + share + k, width), bf16),
        pltpu.VMEM((n_rows, HEAD + share, width), bf16),
        pltpu.VMEM((n_rows, share, 8), f32),
        pltpu.VMEM((n_rows, share, n_cols * share), bf16),
        pltpu.VMEM((n_rows, share, n_cols * share), bf16),
        pltpu.VMEM((k, n_cols * share), bf16),
        pltpu.VMEM((n_cols, 1, share), f32),
        pltpu.VMEM((n_cols, n_cols, 1, share), f32),
        pltpu.VMEM((n_cols, 1, share), f32),
    ] + [pltpu.VMEM((n_rows, k, share), bf16)] * 4
    scratch += [pltpu.VMEM((1, share), f32)]
    scratch += [dma((n, 5))] * 4 + [dma((n_rows, 4))] * 2 + [dma((n_cols,))] * 2
    scratch += [dma((n_rows,))] * 4 + [dma((4,))]
    out = pl.pallas_call(
        functools.partial(kernel, n_rows, n_cols),
        out_shape=pltpu.VMEM((k, share), f32),
        in_specs=[ANY_SPEC, ANY_SPEC, ANY_SPEC],
        out_specs=VMEM_SPEC,
        scratch_shapes=scratch,
        compiler_params=pltpu.CompilerParams(
            collective_id=0, has_side_effects=True, vmem_limit_bytes=58 * 1024 * 1024
        ),
    )(points, spread.reshape(1, share), vectors.T)
    return out.T


def solution(mesh):
    placed = (P(("row", "col"), None), P(("row", "col")), P(("row", "col"), None))
    return jax.shard_map(
        functools.partial(local, mesh.shape["row"], mesh.shape["col"]),
        mesh=mesh, in_specs=placed, out_specs=P(("row", "col"), None), check_vma=False,
    )
```

```python
import functools
import math

import jax
import jax.numpy as jnp
from jax import lax
from jax.experimental import pallas as pl
from jax.experimental.pallas import tpu as pltpu
from jax.sharding import PartitionSpec as P

MESH = pl.DeviceIdType.MESH
LOG2E = math.log2(math.e)
VMEM_SPEC = pl.BlockSpec(memory_space=pltpu.VMEM)
ANY_SPEC = pl.BlockSpec(memory_space=pl.ANY)
HEAD = 16
UNROLL = 8
NT = (((1,), (1,)), ((), ()))


def terms(value):
    high = value.astype(jnp.bfloat16)
    rest = value - high.astype(jnp.float32)
    middle = rest.astype(jnp.bfloat16)
    return [high, middle, (rest - middle.astype(jnp.float32)).astype(jnp.bfloat16)]


def untangle(head):
    head = head.astype(jnp.float32)
    return head[0:1] + head[1:2] + head[2:3], head[3:4] + head[4:5] + head[5:6]


def plan(n_rows, n_cols):
    if (n_rows, n_cols) == (4, 8):
        return [(0, 0), (1, 1), (0, 2), (1, 3)], [(0, 0), (2, 1), (0, 5), (2, 4)], True
    return [(m, 0) for m in range(n_rows)], [(0, 2 * k) for k in range(n_cols // 2)], False


def kernel(
    n_rows, n_cols, pts_ref, bw_ref, vec_ref, out_ref,
    blk, crs, crs_col, direct, mirror, vec_all, part, t_in, inv,
    fwd_out, fwd_in, rev_out, rev_in,
    bw, js, jr, ss, sr, cs, cr, ts, tr, fs, fr, gs, gr, ls,
):
    share, width = pts_ref.shape
    k_vec = vec_ref.shape[0]
    f32, bf16 = jnp.float32, jnp.bfloat16
    firsts, seconds, relayed = plan(n_rows, n_cols)
    half = share // 2
    chunks = [(0, HEAD + half), (HEAD + half, half), (HEAD + share, k_vec), (0, HEAD + share), (0, HEAD + share + k_vec)]
    VECS, WHOLE, ALL = 2, 3, 4
    row = lax.axis_index("row")
    col = lax.axis_index("col")

    def peer(offset):
        return {"row": lax.bitwise_xor(row, offset[0]), "col": lax.bitwise_xor(col, offset[1])}

    def second_at(q):
        return seconds[q // 2][0], seconds[q // 2][1] ^ (q % 2)

    if relayed:
        y, far = row // 2, col // 4
        place = (col + y + far) % 2 + 2 * y + 4 * far
        greeted = [seconds[2], seconds[1], firsts[1], firsts[2], (0, 1)]
    else:
        place = col
        greeted = firsts[1:] + seconds[1:] + [(0, 1)]
    barrier = pltpu.get_barrier_semaphore()
    for offset in greeted:
        pl.semaphore_signal(barrier, inc=1, device_id=peer(offset), device_id_type=MESH)

    loads = [
        pltpu.make_async_copy(pts_ref, crs.at[0, pl.ds(HEAD, share)], ls.at[0]),
        pltpu.make_async_copy(pts_ref, blk.at[0, pl.ds(HEAD, share)], ls.at[1]),
        pltpu.make_async_copy(bw_ref, bw, ls.at[3]),
        pltpu.make_async_copy(vec_ref, blk.at[0, pl.ds(HEAD + share, k_vec)], ls.at[2]),
    ]
    for load in loads:
        load.start()
    loads[0].wait()
    loads[2].wait()
    own = crs[0, HEAD:].astype(f32)
    square = own * own
    high = square.astype(bf16)
    low = (square - high.astype(f32)).astype(bf16)
    halves = jnp.full((8, width), 0.5, bf16)
    wide = lax.dot_general(halves, high, NT, preferred_element_type=f32) + lax.dot_general(
        halves, low, NT, preferred_element_type=f32
    )
    head = jnp.concatenate(
        [t.astype(f32) for t in terms(bw[...] * (2.0 * LOG2E)) + terms(wide[0:1])]
        + [jnp.zeros((HEAD - 6, share), f32)],
        axis=0,
    ).astype(bf16)
    blk[0, 0:HEAD] = head
    crs[0, 0:HEAD] = head
    part[...] = jnp.zeros_like(part)
    loads[1].wait()
    loads[3].wait()
    pl.semaphore_wait(barrier, len(greeted))

    started = []

    def start(copy):
        copy.start()
        started.append(copy)

    def j_copy(src, dst, c, offset):
        rows = pl.ds(*chunks[c])
        return pltpu.make_async_remote_copy(
            src_ref=blk.at[2 * src, rows], dst_ref=blk.at[2 * dst, rows],
            send_sem=js.at[dst, c], recv_sem=jr.at[dst, c],
            device_id=peer(offset), device_id_type=MESH,
        )

    def s_copy(k, c):
        rows = pl.ds(*chunks[c])
        return pltpu.make_async_remote_copy(
            src_ref=blk.at[2 * k, rows], dst_ref=blk.at[2 * k + 1, rows],
            send_sem=ss.at[k, c], recv_sem=sr.at[k, c],
            device_id=peer((0, 1)), device_id_type=MESH,
        )

    def c_copy(src, dst, c, offset):
        rows = pl.ds(*chunks[c])
        return pltpu.make_async_remote_copy(
            src_ref=crs.at[src, rows], dst_ref=crs.at[dst, rows],
            send_sem=cs.at[dst, c], recv_sem=cr.at[dst, c],
            device_id=peer(offset), device_id_type=MESH,
        )

    def j_wait(k, c):
        j_copy(0, k, c, seconds[k]).wait_recv()

    def s_wait(k, c):
        s_copy(k, c).wait_recv()

    def c_wait(m, c):
        c_copy(0, m, c, firsts[m]).wait_recv()

    def column(m):
        spread_row, half_row = untangle(crs[m, 0:HEAD])
        padded = jnp.concatenate([spread_row, half_row, jnp.zeros((6, share), f32)], axis=0)
        crs_col[m] = jnp.transpose(padded)

    everything = (0, share)

    def tile(m, q, i_part=everything, j_part=everything, diagonal=False):
        i0, ni = i_part
        j0, nj = j_part
        cols = crs_col[m, i0 : i0 + ni]
        arow, hrow = untangle(blk[q, 0:HEAD, j0 : j0 + nj])
        cross = lax.dot_general(
            crs[m, HEAD + i0 : HEAD + i0 + ni], blk[q, HEAD + j0 : HEAD + j0 + nj], NT,
            preferred_element_type=f32,
        )
        near = (cross - cols[:, 1:2]) - hrow
        first = jnp.exp2(near * cols[:, 0:1])
        second = jnp.exp2(near * arow)
        if diagonal:
            same = lax.broadcasted_iota(jnp.int32, (ni, nj), 0) == lax.broadcasted_iota(
                jnp.int32, (ni, nj), 1
            )
            first = jnp.where(same, 0.0, first)
            second = jnp.where(same, 0.0, second)
        where = pl.ds(pl.multiple_of(q * share + j0, math.gcd(share, nj)), nj)
        direct[m, i0 : i0 + ni, where] = first.astype(bf16)
        mirror[m, i0 : i0 + ni, where] = second.astype(bf16)
        at = lax.bitwise_xor(place, q)
        part[at, :, j0 : j0 + nj] += jnp.sum(second, axis=0, keepdims=True)

    def tiles(ms, qs, i_part=everything, j_part=everything):
        count = (ms[1] - ms[0]) * (qs[1] - qs[0])

        def body(index, carry):
            tile(ms[0] + index % (ms[1] - ms[0]), qs[0] + index // (ms[1] - ms[0]), i_part, j_part)
            return carry

        lax.fori_loop(0, count, body, 0, unroll=min(count, UNROLL))

    if relayed:
        start(j_copy(0, 2, 0, seconds[2]))
        start(c_copy(0, 2, 0, firsts[2]))
        start(j_copy(0, 1, ALL, seconds[1]))
        start(c_copy(0, 1, WHOLE, firsts[1]))
        start(s_copy(0, ALL))
        start(j_copy(0, 2, 1, seconds[2]))
        start(c_copy(0, 2, 1, firsts[2]))
        column(0)
        tile(0, 0, diagonal=True)
        s_wait(0, ALL)
        tile(0, 1)
        for c in (0, 1):
            j_wait(2, c)
            start(j_copy(2, 3, c, seconds[1]))
            c_wait(2, c)
            start(c_copy(2, 3, c, firsts[1]))
            start(s_copy(2, c))
            if c == 0:
                j_wait(1, ALL)
                start(s_copy(1, ALL))
                c_wait(1, WHOLE)
                start(j_copy(0, 2, VECS, seconds[2]))
                column(1)
                tiles((1, 2), (0, 2))
                tiles((0, 2), (2, 3))
                s_wait(1, ALL)
                tiles((0, 2), (3, 4))
        column(2)
        tiles((2, 3), (0, 4))
        tiles((0, 3), (4, 5))
        s_wait(2, 0)
        s_wait(2, 1)
        tiles((0, 3), (5, 6))
        j_wait(2, VECS)
        start(j_copy(2, 3, VECS, seconds[1]))
        start(s_copy(2, VECS))
        for c in (0, 1):
            piece = (c * half, half)
            j_wait(3, c)
            start(s_copy(3, c))
            tiles((0, 3), (6, 7), j_part=piece)
            c_wait(3, c)
            if c == 0:
                column(3)
            tiles((3, 4), (0, 6), i_part=piece)
            if c == 1:
                tile(3, 6)
            s_wait(3, c)
            tiles((0, 3), (7, 8), j_part=piece)
        tile(3, 7)
        late = [2, 3]
    else:
        for k in range(1, len(seconds)):
            start(j_copy(0, k, WHOLE, seconds[k]))
        for m in range(1, n_rows):
            start(c_copy(0, m, WHOLE, firsts[m]))
        start(s_copy(0, ALL))
        column(0)
        tile(0, 0, diagonal=True)
        s_wait(0, ALL)
        tile(0, 1)
        for m in range(1, n_rows):
            c_wait(m, WHOLE)
            column(m)
        tiles((1, n_rows), (0, 2))
        for k in range(1, len(seconds)):
            j_wait(k, WHOLE)
            start(s_copy(k, WHOLE))
            start(j_copy(0, k, VECS, seconds[k]))
            tiles((0, n_rows), (2 * k, 2 * k + 1))
            s_wait(k, WHOLE)
            tiles((0, n_rows), (2 * k + 1, 2 * k + 2))
        late = list(range(1, len(seconds)))

    totals = []
    for x in range(n_cols - 1, 0, -1):
        copy = pltpu.make_async_remote_copy(
            src_ref=part, dst_ref=t_in.at[x], send_sem=ts.at[x], recv_sem=tr.at[x],
            device_id=peer(second_at(x)), device_id_type=MESH,
        )
        start(copy)
        totals.insert(0, copy)
    if not relayed:
        for k in late:
            j_wait(k, VECS)
            start(s_copy(k, VECS))
    if relayed:
        j_wait(3, VECS)
        start(s_copy(3, VECS))
    for k in late:
        s_wait(k, VECS)
    for q in range(n_cols):
        vec_all[:, q * share : (q + 1) * share] = blk[q, HEAD + share :]

    def reduce_send(m, value, out, in_, send, recv):
        out[m] = value.astype(bf16)
        copy = pltpu.make_async_remote_copy(
            src_ref=out.at[m], dst_ref=in_.at[m], send_sem=send.at[m], recv_sem=recv.at[m],
            device_id=peer(firsts[m]), device_id_type=MESH,
        )
        start(copy)
        return copy

    def product(left, right):
        return lax.dot_general(left, right, NT, preferred_element_type=f32)

    order = list(range(n_rows - 1, 0, -1))
    fwd = {m: reduce_send(m, product(vec_all[...], direct[m]), fwd_out, fwd_in, fs, fr) for m in order}
    forward = product(vec_all[...], direct[0])

    total = part[...]
    for x in range(1, n_cols):
        totals[x - 1].wait_recv()
        total = total + t_in[x]
    inv[...] = 0.125 / total
    scaled = jnp.concatenate(
        [
            (vec_all[:, q * share : (q + 1) * share].astype(f32) * inv[lax.bitwise_xor(place, q)]).astype(bf16)
            for q in range(n_cols)
        ],
        axis=1,
    )
    rev = {m: reduce_send(m, product(scaled, mirror[m]), rev_out, rev_in, gs, gr) for m in order}
    reverse = product(scaled, mirror[0])
    for m in range(1, n_rows):
        fwd[m].wait_recv()
        forward = forward + fwd_in[m].astype(f32)
    forward = forward * inv[place]
    for copy in started:
        copy.wait_send()
    for m in range(1, n_rows):
        rev[m].wait_recv()
        reverse = reverse + rev_in[m].astype(f32)
    out_ref[...] = 4.0 * (forward + reverse)


def local(n_rows, n_cols, points, spread, vectors):
    share, width = points.shape
    k = vectors.shape[1]
    f32, bf16 = jnp.float32, jnp.bfloat16
    dma = pltpu.SemaphoreType.DMA
    n = n_cols // 2
    scratch = [
        pltpu.VMEM((n_cols, HEAD + share + k, width), bf16),
        pltpu.VMEM((n_rows, HEAD + share, width), bf16),
        pltpu.VMEM((n_rows, share, 8), f32),
        pltpu.VMEM((n_rows, share, n_cols * share), bf16),
        pltpu.VMEM((n_rows, share, n_cols * share), bf16),
        pltpu.VMEM((k, n_cols * share), bf16),
        pltpu.VMEM((n_cols, 1, share), f32),
        pltpu.VMEM((n_cols, n_cols, 1, share), f32),
        pltpu.VMEM((n_cols, 1, share), f32),
    ] + [pltpu.VMEM((n_rows, k, share), bf16)] * 4
    scratch += [pltpu.VMEM((1, share), f32)]
    scratch += [dma((n, 5))] * 4 + [dma((n_rows, 4))] * 2 + [dma((n_cols,))] * 2
    scratch += [dma((n_rows,))] * 4 + [dma((4,))]
    out = pl.pallas_call(
        functools.partial(kernel, n_rows, n_cols),
        out_shape=pltpu.VMEM((k, share), f32),
        in_specs=[ANY_SPEC, ANY_SPEC, ANY_SPEC],
        out_specs=VMEM_SPEC,
        scratch_shapes=scratch,
        compiler_params=pltpu.CompilerParams(
            collective_id=0, has_side_effects=True, vmem_limit_bytes=58 * 1024 * 1024
        ),
    )(points, spread.reshape(1, share), vectors.T)
    return out.T


def solution(mesh):
    placed = (P(("row", "col"), None), P(("row", "col")), P(("row", "col"), None))
    return jax.shard_map(
        functools.partial(local, mesh.shape["row"], mesh.shape["col"]),
        mesh=mesh, in_specs=placed, out_specs=P(("row", "col"), None), check_vma=False,
    )
```

```python
import functools
import math

import jax
import jax.numpy as jnp
from jax import lax
from jax.experimental import pallas as pl
from jax.experimental.pallas import tpu as pltpu
from jax.sharding import PartitionSpec as P

MESH = pl.DeviceIdType.MESH
LOG2E = math.log2(math.e)
VMEM_SPEC = pl.BlockSpec(memory_space=pltpu.VMEM)
ANY_SPEC = pl.BlockSpec(memory_space=pl.ANY)
HEAD = 16
UNROLL = 8
NT = (((1,), (1,)), ((), ()))


def terms(value):
    high = value.astype(jnp.bfloat16)
    rest = value - high.astype(jnp.float32)
    middle = rest.astype(jnp.bfloat16)
    return [high, middle, (rest - middle.astype(jnp.float32)).astype(jnp.bfloat16)]


def untangle(head):
    head = head.astype(jnp.float32)
    return head[0:1] + head[1:2] + head[2:3], head[3:4] + head[4:5] + head[5:6]


def plan(n_rows, n_cols):
    if (n_rows, n_cols) == (4, 8):
        return [(0, 0), (1, 1), (0, 2), (1, 3)], [(0, 0), (2, 1), (0, 4), (2, 5)], True
    return [(m, 0) for m in range(n_rows)], [(0, 2 * k) for k in range(n_cols // 2)], False


def kernel(
    n_rows, n_cols, pts_ref, bw_ref, vec_ref, out_ref,
    blk, crs, crs_col, direct, mirror, vec_all, part, t_in, inv,
    fwd_out, fwd_in, rev_out, rev_in,
    bw, js, jr, ss, sr, cs, cr, ts, tr, fs, fr, gs, gr, ls,
):
    share, width = pts_ref.shape
    k_vec = vec_ref.shape[0]
    f32, bf16 = jnp.float32, jnp.bfloat16
    firsts, seconds, relayed = plan(n_rows, n_cols)
    half = share // 2
    chunks = [(0, HEAD + half), (HEAD + half, half), (HEAD + share, k_vec), (0, HEAD + share), (0, HEAD + share + k_vec)]
    VECS, WHOLE, ALL = 2, 3, 4
    row = lax.axis_index("row")
    col = lax.axis_index("col")

    def peer(offset):
        return {"row": lax.bitwise_xor(row, offset[0]), "col": lax.bitwise_xor(col, offset[1])}

    def second_at(q):
        return seconds[q // 2][0], seconds[q // 2][1] ^ (q % 2)

    if relayed:
        y, far = row // 2, col // 4
        place = (col + y) % 2 + 2 * y + 4 * far
        greeted = [seconds[2], seconds[1], firsts[1], firsts[2], (0, 1)]
    else:
        place = col
        greeted = firsts[1:] + seconds[1:] + [(0, 1)]
    barrier = pltpu.get_barrier_semaphore()
    for offset in greeted:
        pl.semaphore_signal(barrier, inc=1, device_id=peer(offset), device_id_type=MESH)

    loads = [
        pltpu.make_async_copy(pts_ref, crs.at[0, pl.ds(HEAD, share)], ls.at[0]),
        pltpu.make_async_copy(pts_ref, blk.at[0, pl.ds(HEAD, share)], ls.at[1]),
        pltpu.make_async_copy(bw_ref, bw, ls.at[3]),
        pltpu.make_async_copy(vec_ref, blk.at[0, pl.ds(HEAD + share, k_vec)], ls.at[2]),
    ]
    for load in loads:
        load.start()
    loads[0].wait()
    loads[2].wait()
    own = crs[0, HEAD:].astype(f32)
    square = own * own
    high = square.astype(bf16)
    low = (square - high.astype(f32)).astype(bf16)
    halves = jnp.full((8, width), 0.5, bf16)
    wide = lax.dot_general(halves, high, NT, preferred_element_type=f32) + lax.dot_general(
        halves, low, NT, preferred_element_type=f32
    )
    head = jnp.concatenate(
        [t.astype(f32) for t in terms(bw[...] * (2.0 * LOG2E)) + terms(wide[0:1])]
        + [jnp.zeros((HEAD - 6, share), f32)],
        axis=0,
    ).astype(bf16)
    blk[0, 0:HEAD] = head
    crs[0, 0:HEAD] = head
    part[...] = jnp.zeros_like(part)
    loads[1].wait()
    loads[3].wait()
    pl.semaphore_wait(barrier, len(greeted))

    started = []

    def start(copy):
        copy.start()
        started.append(copy)

    def j_copy(src, dst, c, offset):
        rows = pl.ds(*chunks[c])
        return pltpu.make_async_remote_copy(
            src_ref=blk.at[2 * src, rows], dst_ref=blk.at[2 * dst, rows],
            send_sem=js.at[dst, c], recv_sem=jr.at[dst, c],
            device_id=peer(offset), device_id_type=MESH,
        )

    def s_copy(k, c):
        rows = pl.ds(*chunks[c])
        return pltpu.make_async_remote_copy(
            src_ref=blk.at[2 * k, rows], dst_ref=blk.at[2 * k + 1, rows],
            send_sem=ss.at[k, c], recv_sem=sr.at[k, c],
            device_id=peer((0, 1)), device_id_type=MESH,
        )

    def c_copy(src, dst, c, offset):
        rows = pl.ds(*chunks[c])
        return pltpu.make_async_remote_copy(
            src_ref=crs.at[src, rows], dst_ref=crs.at[dst, rows],
            send_sem=cs.at[dst, c], recv_sem=cr.at[dst, c],
            device_id=peer(offset), device_id_type=MESH,
        )

    def j_wait(k, c):
        j_copy(0, k, c, seconds[k]).wait_recv()

    def s_wait(k, c):
        s_copy(k, c).wait_recv()

    def c_wait(m, c):
        c_copy(0, m, c, firsts[m]).wait_recv()

    def column(m):
        spread_row, half_row = untangle(crs[m, 0:HEAD])
        padded = jnp.concatenate([spread_row, half_row, jnp.zeros((6, share), f32)], axis=0)
        crs_col[m] = jnp.transpose(padded)

    everything = (0, share)

    def tile(m, q, i_part=everything, j_part=everything, diagonal=False):
        i0, ni = i_part
        j0, nj = j_part
        cols = crs_col[m, i0 : i0 + ni]
        arow, hrow = untangle(blk[q, 0:HEAD, j0 : j0 + nj])
        cross = lax.dot_general(
            crs[m, HEAD + i0 : HEAD + i0 + ni], blk[q, HEAD + j0 : HEAD + j0 + nj], NT,
            preferred_element_type=f32,
        )
        near = (cross - cols[:, 1:2]) - hrow
        first = jnp.exp2(near * cols[:, 0:1])
        second = jnp.exp2(near * arow)
        if diagonal:
            same = lax.broadcasted_iota(jnp.int32, (ni, nj), 0) == lax.broadcasted_iota(
                jnp.int32, (ni, nj), 1
            )
            first = jnp.where(same, 0.0, first)
            second = jnp.where(same, 0.0, second)
        where = pl.ds(pl.multiple_of(q * share + j0, math.gcd(share, nj)), nj)
        direct[m, i0 : i0 + ni, where] = first.astype(bf16)
        mirror[m, i0 : i0 + ni, where] = second.astype(bf16)
        at = lax.bitwise_xor(place, q)
        part[at, :, j0 : j0 + nj] += jnp.sum(second, axis=0, keepdims=True)

    def tiles(ms, qs, i_part=everything, j_part=everything):
        count = (ms[1] - ms[0]) * (qs[1] - qs[0])

        def body(index, carry):
            tile(ms[0] + index % (ms[1] - ms[0]), qs[0] + index // (ms[1] - ms[0]), i_part, j_part)
            return carry

        lax.fori_loop(0, count, body, 0, unroll=min(count, UNROLL))

    if relayed:
        start(j_copy(0, 2, 0, seconds[2]))
        start(c_copy(0, 2, 0, firsts[2]))
        start(j_copy(0, 1, ALL, seconds[1]))
        start(c_copy(0, 1, WHOLE, firsts[1]))
        start(s_copy(0, ALL))
        start(j_copy(0, 2, 1, seconds[2]))
        start(c_copy(0, 2, 1, firsts[2]))
        column(0)
        tile(0, 0, diagonal=True)
        s_wait(0, ALL)
        tile(0, 1)
        for c in (0, 1):
            j_wait(2, c)
            start(j_copy(2, 3, c, seconds[1]))
            c_wait(2, c)
            start(c_copy(2, 3, c, firsts[1]))
            start(s_copy(2, c))
            if c == 0:
                j_wait(1, ALL)
                start(s_copy(1, ALL))
                c_wait(1, WHOLE)
                start(j_copy(0, 2, VECS, seconds[2]))
                column(1)
                tiles((1, 2), (0, 2))
                tiles((0, 2), (2, 3))
                s_wait(1, ALL)
                tiles((0, 2), (3, 4))
        column(2)
        tiles((2, 3), (0, 4))
        tiles((0, 3), (4, 5))
        s_wait(2, 0)
        s_wait(2, 1)
        tiles((0, 3), (5, 6))
        j_wait(2, VECS)
        start(j_copy(2, 3, VECS, seconds[1]))
        start(s_copy(2, VECS))
        for c in (0, 1):
            piece = (c * half, half)
            j_wait(3, c)
            start(s_copy(3, c))
            tiles((0, 3), (6, 7), j_part=piece)
            c_wait(3, c)
            if c == 0:
                column(3)
            tiles((3, 4), (0, 6), i_part=piece)
            if c == 1:
                tile(3, 6)
            s_wait(3, c)
            tiles((0, 3), (7, 8), j_part=piece)
        tile(3, 7)
        late = [2, 3]
    else:
        for k in range(1, len(seconds)):
            start(j_copy(0, k, WHOLE, seconds[k]))
        for m in range(1, n_rows):
            start(c_copy(0, m, WHOLE, firsts[m]))
        start(s_copy(0, ALL))
        column(0)
        tile(0, 0, diagonal=True)
        s_wait(0, ALL)
        tile(0, 1)
        for m in range(1, n_rows):
            c_wait(m, WHOLE)
            column(m)
        tiles((1, n_rows), (0, 2))
        for k in range(1, len(seconds)):
            j_wait(k, WHOLE)
            start(s_copy(k, WHOLE))
            start(j_copy(0, k, VECS, seconds[k]))
            tiles((0, n_rows), (2 * k, 2 * k + 1))
            s_wait(k, WHOLE)
            tiles((0, n_rows), (2 * k + 1, 2 * k + 2))
        late = list(range(1, len(seconds)))

    totals = []
    for x in range(n_cols - 1, 0, -1):
        copy = pltpu.make_async_remote_copy(
            src_ref=part, dst_ref=t_in.at[x], send_sem=ts.at[x], recv_sem=tr.at[x],
            device_id=peer(second_at(x)), device_id_type=MESH,
        )
        start(copy)
        totals.insert(0, copy)
    if not relayed:
        for k in late:
            j_wait(k, VECS)
            start(s_copy(k, VECS))
    if relayed:
        j_wait(3, VECS)
        start(s_copy(3, VECS))
    for k in late:
        s_wait(k, VECS)
    for q in range(n_cols):
        vec_all[:, q * share : (q + 1) * share] = blk[q, HEAD + share :]

    def reduce_send(m, value, out, in_, send, recv):
        out[m] = value.astype(bf16)
        copy = pltpu.make_async_remote_copy(
            src_ref=out.at[m], dst_ref=in_.at[m], send_sem=send.at[m], recv_sem=recv.at[m],
            device_id=peer(firsts[m]), device_id_type=MESH,
        )
        start(copy)
        return copy

    def product(left, right):
        return lax.dot_general(left, right, NT, preferred_element_type=f32)

    order = list(range(n_rows - 1, 0, -1))
    fwd = {m: reduce_send(m, product(vec_all[...], direct[m]), fwd_out, fwd_in, fs, fr) for m in order}
    forward = product(vec_all[...], direct[0])

    total = part[...]
    for x in range(1, n_cols):
        totals[x - 1].wait_recv()
        total = total + t_in[x]
    inv[...] = 0.125 / total
    scaled = jnp.concatenate(
        [
            (vec_all[:, q * share : (q + 1) * share].astype(f32) * inv[lax.bitwise_xor(place, q)]).astype(bf16)
            for q in range(n_cols)
        ],
        axis=1,
    )
    rev = {m: reduce_send(m, product(scaled, mirror[m]), rev_out, rev_in, gs, gr) for m in order}
    reverse = product(scaled, mirror[0])
    for m in range(1, n_rows):
        fwd[m].wait_recv()
        forward = forward + fwd_in[m].astype(f32)
    forward = forward * inv[place]
    for copy in started:
        copy.wait_send()
    for m in range(1, n_rows):
        rev[m].wait_recv()
        reverse = reverse + rev_in[m].astype(f32)
    out_ref[...] = 4.0 * (forward + reverse)


def local(n_rows, n_cols, points, spread, vectors):
    share, width = points.shape
    k = vectors.shape[1]
    f32, bf16 = jnp.float32, jnp.bfloat16
    dma = pltpu.SemaphoreType.DMA
    n = n_cols // 2
    scratch = [
        pltpu.VMEM((n_cols, HEAD + share + k, width), bf16),
        pltpu.VMEM((n_rows, HEAD + share, width), bf16),
        pltpu.VMEM((n_rows, share, 8), f32),
        pltpu.VMEM((n_rows, share, n_cols * share), bf16),
        pltpu.VMEM((n_rows, share, n_cols * share), bf16),
        pltpu.VMEM((k, n_cols * share), bf16),
        pltpu.VMEM((n_cols, 1, share), f32),
        pltpu.VMEM((n_cols, n_cols, 1, share), f32),
        pltpu.VMEM((n_cols, 1, share), f32),
    ] + [pltpu.VMEM((n_rows, k, share), bf16)] * 4
    scratch += [pltpu.VMEM((1, share), f32)]
    scratch += [dma((n, 5))] * 4 + [dma((n_rows, 4))] * 2 + [dma((n_cols,))] * 2
    scratch += [dma((n_rows,))] * 4 + [dma((4,))]
    out = pl.pallas_call(
        functools.partial(kernel, n_rows, n_cols),
        out_shape=pltpu.VMEM((k, share), f32),
        in_specs=[ANY_SPEC, ANY_SPEC, ANY_SPEC],
        out_specs=VMEM_SPEC,
        scratch_shapes=scratch,
        compiler_params=pltpu.CompilerParams(
            collective_id=0, has_side_effects=True, vmem_limit_bytes=58 * 1024 * 1024
        ),
    )(points, spread.reshape(1, share), vectors.T)
    return out.T


def solution(mesh):
    placed = (P(("row", "col"), None), P(("row", "col")), P(("row", "col"), None))
    return jax.shard_map(
        functools.partial(local, mesh.shape["row"], mesh.shape["col"]),
        mesh=mesh, in_specs=placed, out_specs=P(("row", "col"), None), check_vma=False,
    )
```
